256 devices in a mesh: owner: 8 (over y, core), group: 32 (over z, x).
Axes of the slice: x: 4, y: 4, z: 8, core: 2. Of those that a mesh axis runs over, the one named last changes fastest.
Arguments:
- amplitudes: bfloat16 [1024, 32768], P('group', 'owner'), may hold values from -6 to 6
- integrals: bfloat16 [32768, 32768], P('owner', 'group'), may hold values from -0.09375 to 0.09375
- occ_irrep: int32 [100], replicated, may hold values from 0 to 7
- vir_irrep: int32 [1200], replicated, may hold values from 0 to 7, as said below
- cd_list: int32 [2, 32768], P(None, 'owner'), may hold values from 0 to 1199
- ab_list: int32 [2, 32768], P(None, 'group'), may hold values from 0 to 1199, as said below
Outputs:
- ladder: bfloat16 [1024, 32768], P('owner', 'group')
The draws below stay inside these ranges and needn't reach their ends.
Inputs may be any that keep to these rules, and one draw needn't show every extreme that they name: `vir_irrep`: irrep labels of D2h; each of the 8 labels occurs. `occ_irrep`: irrep labels of D2h. `cd_list`: indices of virtual orbitals. `ab_list`: indices of virtual orbitals; the residual pairs of each index of group form 8 consecutive blocks of 128 pairs, and every pair (a,b) of block k has vir_irrep[a] XOR vir_irrep[b] == k.
All inputs are finite; a program needn't handle non-finite values.
Results may differ from the reference program's by a relative error of at most 0.001.
Values may be sent and summed in bfloat16 or wider, within the bound.
No kernel may reach another device: no remote copies, remote signals or barrier semaphores. Data moves between devices by JAX's collectives and lax.ppermute only.
A program may use at most 64 MiB of HBM per device.

```python
import jax
import jax.numpy as jnp
from jax import lax

NO = 100
NV = 1200
AB_DEV = 1024
PAIRS = 1024
CD = 32768
AB = 32768
N_GROUP = 32


def orbital_irreps(key):
    base = jax.random.fold_in(key, 11)
    first = jax.random.permutation(jax.random.fold_in(base, 1), 8).astype(jnp.int32)
    rest = jax.random.randint(jax.random.fold_in(base, 2), (NV,), 0, 8).astype(jnp.int32)
    index = jnp.arange(NV, dtype=jnp.int32)
    return jnp.where(index < 8, first[jnp.minimum(index, 7)], rest)


def draw_vir_irrep(key, part):
    return orbital_irreps(key)


def draw_ab_list(key, part):
    labels = orbital_irreps(key)
    order = jnp.argsort(labels, stable=True).astype(jnp.int32)
    counts = jnp.sum((labels[None, :] == jnp.arange(8, dtype=jnp.int32)[:, None]).astype(jnp.int32), axis=1)
    starts = jnp.cumsum(counts) - counts
    column = jnp.arange(AB, dtype=jnp.int32)
    target = column % AB_DEV // (AB_DEV // 8)
    first = jax.random.randint(jax.random.fold_in(key, 21), (AB,), 0, NV).astype(jnp.int32)
    wanted = jnp.bitwise_xor(labels[first], target)
    pick = jax.random.randint(jax.random.fold_in(key, 22), (AB,), 0, 1 << 20).astype(jnp.int32)
    second = order[starts[wanted] + pick % counts[wanted]]
    return jnp.stack([first, second]).astype(jnp.int32)


def with_ends(entries, key, smallest, high):
    spot = [jax.random.randint(jax.random.fold_in(key, axis), (), 0, length) for axis, length in enumerate(entries.shape)]
    main_axis = entries.shape.index(max(entries.shape))
    next_to = spot[:main_axis] + [(spot[main_axis] + 1) % entries.shape[main_axis]] + spot[main_axis + 1:]
    return entries.at[tuple(spot)].set(smallest).at[tuple(next_to)].set(high)


def strengthened(array, rng, source, target, parts, factor):
    owner, partner = [(jnp.arange(array.shape[dim]) // (array.shape[dim] // parts)).reshape([-1 if axis == dim else 1 for axis in range(array.ndim)]) for dim in (source, target)]
    chosen = jax.random.permutation(rng, parts)[partner]
    strong = (owner == chosen) | (owner == (partner + parts // 2) % parts)
    return jnp.where(strong, factor * array, array)


def block_scale(stream_key, dims, shards, low, largest):
    factor_of = 1.0
    for position, shards_of in shards:
        draws = jax.random.uniform(jax.random.fold_in(jax.random.fold_in(stream_key, 6), position), (shards_of,), jnp.float32, low / len(shards), largest / len(shards))
        factor_of = factor_of * jnp.repeat(jnp.exp(draws), dims[position] // shards_of).reshape((-1,) + (1,) * (len(dims) - 1 - position))
    return factor_of


def noise(key, extent, deviation, reach, shards=(), held_as=jnp.bfloat16):
    level = block_scale(key, extent, shards, -0.22, 0.18) if shards else 1.0
    entries = jax.random.normal(key, extent, jnp.float32) * deviation * level
    return jnp.minimum(jnp.maximum(entries, -reach), reach).astype(held_as)


def heavy_noise(rng, dims, deviation, bound, split, heavy, held_as=jnp.bfloat16):
    result = deviation * jax.random.normal(rng, dims, jnp.float32)
    if split:
        result = result * block_scale(rng, dims, split, -0.22, 0.18)
    return jnp.clip(strengthened(result, jax.random.fold_in(rng, 3), *heavy), -bound, bound).astype(held_as)


def setup_inputs(seed: int = 0) -> dict:
    arg_keys = jax.random.split(jax.random.key(seed), 7)
    amplitudes = heavy_noise(arg_keys[0], (PAIRS, CD), 1.0, 6.0, ((0, 32), (1, 8)), (1, 0, 32, 2.75))
    integrals = noise(arg_keys[1], (CD, AB), (CD // 8) ** -0.5, 0.09375, ((0, 8), (1, 32)))
    occ_irrep = with_ends(jax.random.randint(arg_keys[2], (NO,), 0, 8), jax.random.fold_in(arg_keys[2], 1), 0, 7).astype(jnp.int32)
    vir_irrep = draw_vir_irrep(jax.random.fold_in(arg_keys[6], 71), 0)
    cd_list = with_ends(jax.random.randint(arg_keys[4], (2, CD), 0, NV), jax.random.fold_in(arg_keys[4], 1), 0, NV - 1).astype(jnp.int32)
    ab_list = draw_ab_list(jax.random.fold_in(arg_keys[6], 71), 0)
    return dict(amplitudes=amplitudes, integrals=integrals, occ_irrep=occ_irrep, vir_irrep=vir_irrep, cd_list=cd_list, ab_list=ab_list)


def pair_irreps(pair_list, table):
    return jnp.bitwise_xor(jnp.take(table, pair_list[0], axis=0), jnp.take(table, pair_list[1], axis=0))


def reference(amplitudes, integrals, occ_irrep, vir_irrep, cd_list, ab_list):
    sym_cd = pair_irreps(cd_list, vir_irrep)
    sym_ab = pair_irreps(ab_list, vir_irrep)
    rows = jnp.arange(PAIRS, dtype=jnp.int32)
    sym_ij = jnp.bitwise_xor(jnp.take(occ_irrep, rows // NO, axis=0), jnp.take(occ_irrep, rows % NO, axis=0))
    t_sym = jnp.where(sym_ij[:, None] == sym_cd[None, :], amplitudes, jnp.zeros((), amplitudes.dtype))

    def column_block(index):
        start = (index * AB_DEV).astype(jnp.int32)
        weights = lax.dynamic_slice_in_dim(integrals, start, AB_DEV, 1)
        sym_cols = lax.dynamic_slice_in_dim(sym_ab, start, AB_DEV, 0)
        weights = jnp.where(sym_cd[:, None] == sym_cols[None, :], weights, jnp.zeros((), weights.dtype))
        return jnp.dot(t_sym, weights, preferred_element_type=jnp.float32).astype(jnp.bfloat16)

    blocks = lax.map(column_block, jnp.arange(N_GROUP, dtype=jnp.int32))
    return jnp.transpose(blocks, (1, 0, 2)).reshape(PAIRS, AB)
```

```python
import functools

import jax
import jax.numpy as jnp
from jax import lax
from jax.experimental import pallas as pl
from jax.experimental.pallas import tpu as pltpu
from jax.sharding import Mesh, PartitionSpec as P


LANES = 128
CLASSES = 8
SLOTS = 640
F32, BF16, I32 = jnp.float32, jnp.bfloat16, jnp.int32
VMEM = pl.BlockSpec(memory_space=pltpu.VMEM)
SMEM = pl.BlockSpec(memory_space=pltpu.SMEM)


def iota(shape, dim):
    return lax.broadcasted_iota(I32, shape, dim)


def row_classes(occ_row, first, rows, n_occ):
    r = first + iota((rows, LANES), 0)
    i = jnp.zeros_like(r)
    for m in range(1, 11):
        i = i + (r >= m * n_occ).astype(I32)
    j = r - i * n_occ
    lane = iota((rows, LANES), 1)
    occ = jnp.broadcast_to(occ_row, (rows, LANES))
    a = jnp.sum(jnp.where(lane == i, occ, 0), axis=1, keepdims=True)
    b = jnp.sum(jnp.where(lane == j, occ, 0), axis=1, keepdims=True)
    return jnp.bitwise_xor(a, b)


def pack_kernel(n_occ, n_vir, start, occ_ref, vir_ref, cd_ref, amp_ref, t_ref, hot_ref, symt_ref, cnt_ref, occ_s, vir_s, idx_s):
    rows, pairs = amp_ref.shape
    chunks = pairs // LANES
    occ_s[...] = jnp.zeros_like(occ_s)
    occ_s[:, :n_occ] = occ_ref[...]
    vir_s[...] = jnp.zeros_like(vir_s)
    vir_s[:, :n_vir] = vir_ref[...]
    for m in range(chunks):
        for k in range(2):
            idx_s[k * chunks + m : k * chunks + m + 1, :] = cd_ref[k : k + 1, m * LANES : (m + 1) * LANES]
    words = []
    for w in range(2):
        word = jnp.zeros((1, LANES), I32)
        for k in range(8):
            at = (w * 8 + k) * LANES
            if at < n_vir:
                word = word | (vir_s[:, at : at + LANES] << (4 * k))
        words.append(word)
    idx = idx_s[...]
    low, high = idx & (LANES - 1), idx >> 7
    found = [
        jnp.take_along_axis(jnp.broadcast_to(w, idx.shape), low, axis=1, mode="promise_in_bounds") for w in words
    ]
    label = lax.shift_right_logical(jnp.where(high < 8, found[0], found[1]), (high & 7) * 4) & 7
    sym = jnp.bitwise_xor(label[:chunks], label[chunks:])

    hot = jnp.concatenate([(sym == g).astype(F32) for g in range(CLASSES)], axis=0).astype(BF16)
    before = (iota((LANES, LANES), 0) < iota((LANES, LANES), 1)).astype(F32).astype(BF16)
    inside = jnp.dot(hot, before, preferred_element_type=F32)
    total = jnp.dot(hot, jnp.ones((LANES, LANES), BF16), preferred_element_type=F32)
    earlier = (iota((chunks, chunks), 1) < iota((chunks, chunks), 0)).astype(F32).astype(BF16)
    slot = jnp.zeros((chunks, LANES), F32)
    most = jnp.zeros((1, LANES), F32)
    for g in range(CLASSES):
        part = slice(g * chunks, (g + 1) * chunks)
        base = jnp.dot(earlier, total[part].astype(BF16), preferred_element_type=F32)
        slot = jnp.where(sym == g, inside[part] + base, slot)
        most = jnp.maximum(most, (base + total[part])[chunks - 1 :, :])
    cnt_ref[...] = jnp.broadcast_to(most, cnt_ref.shape)
    slot = slot.astype(I32) - start[0]
    wide = jnp.concatenate([sym, jnp.zeros((LANES - chunks, LANES), I32)], axis=0).astype(F32)
    symt_ref[...] = wide.T

    gidx = lax.axis_index("z") * 4 + lax.axis_index("x")
    cls = row_classes(occ_s[...], gidx * rows, rows, n_occ)
    acc = jnp.zeros((rows, SLOTS), F32)
    step = 2 * LANES
    for m in range(pairs // step):
        s = jnp.concatenate([slot[2 * m : 2 * m + 1], slot[2 * m + 1 : 2 * m + 2]], axis=1)
        y = jnp.concatenate([sym[2 * m : 2 * m + 1], sym[2 * m + 1 : 2 * m + 2]], axis=1)
        one = (iota((SLOTS, step), 0) == s).astype(F32).astype(BF16)
        hot_ref[:, m * step : (m + 1) * step] = one
        amp = amp_ref[:, m * step : (m + 1) * step].astype(F32)
        kept = jnp.where(cls == y, amp, 0.0).astype(BF16)
        acc = acc + lax.dot_general(kept, one, (((1,), (1,)), ((), ())), preferred_element_type=F32)
    t_ref[...] = acc.astype(BF16)


def weights_kernel(part, hot_ref, symt_ref, w_ref, out_ref, kept):
    width = out_ref.shape[1]
    lane_class = part * (width // LANES) + iota((LANES, width), 1) // LANES
    for m in range(w_ref.shape[0] // LANES):
        sym = symt_ref[:, m : m + 1].astype(I32)
        w = w_ref[m * LANES : (m + 1) * LANES, :].astype(F32)
        kept[m * LANES : (m + 1) * LANES, :] = jnp.where(lane_class == sym, w, 0.0).astype(BF16)
    out_ref[...] = jnp.dot(hot_ref[...], kept[...], preferred_element_type=F32).astype(BF16)


def product_kernel(n_occ, places, occ_ref, cnt_ref, *refs):
    n = len(places)
    blocks, weights = refs[:n], refs[n:-5]
    keep_ref, send_ref, rows_s, sums_s, occ_s = refs[-5:]
    z, x = lax.axis_index("z"), lax.axis_index("x")
    y, core = lax.axis_index("y"), lax.axis_index("core")
    for ref, (dz, order) in zip(blocks, places):
        for j, dx in enumerate(order):
            at = ((z + dz) % 8) * 128 + ((x + dx) % 4) * 32
            rows_s[pl.ds(pl.multiple_of(at, 32), 32), :] = ref[j * 32 : (j + 1) * 32, :]
    occ_s[...] = jnp.zeros_like(occ_s)
    occ_s[:, :n_occ] = occ_ref[...]
    height = 256
    for h in range(rows_s.shape[0] // height):
        cls = row_classes(occ_s[...], h * height, height, n_occ)
        total = jnp.zeros((height, LANES), F32)
        for p, w in enumerate(weights):
            out = jnp.dot(rows_s[h * height : (h + 1) * height, :], w[...], preferred_element_type=F32)
            for q in range(w.shape[1] // LANES):
                g = p * (w.shape[1] // LANES) + q
                total = total + jnp.where(cls == g, out[:, q * LANES : (q + 1) * LANES], 0.0)
        for b in range(height // 128):
            sums_s[h * (height // 128) + b] = total[b * 128 : (b + 1) * 128]
    for k in range(4):
        keep_ref[k, :128] = sums_s[2 * k + core]
        send_ref[k, :128] = sums_s[2 * k + 1 - core]
        keep_ref[k, 128:] = cnt_ref[...]
        send_ref[k, 128:] = cnt_ref[...]


def fold_kernel(keep_ref, got_ref, *outs):
    y = lax.axis_index("y")
    for k, out in enumerate(outs):
        at = (y + k) % 4
        out[:128] = keep_ref[at, :128] + got_ref[at, :128]
        out[128:] = jnp.maximum(keep_ref[at, 128:], got_ref[at, 128:])


def finish_kernel(n_occ, occ_ref, prev_ref, a, b, c, d, out_ref, sum_ref, most_ref, occ_s):
    first = (lax.axis_index("y") * 2 + lax.axis_index("core")) * 128
    occ_s[...] = jnp.zeros_like(occ_s)
    occ_s[:, :n_occ] = occ_ref[...]
    cls = row_classes(occ_s[...], first, 128, n_occ)
    total = (a[:128] + b[:128]) + (c[:128] + d[:128])
    if prev_ref is not None:
        total = total + prev_ref[...]
    sum_ref[...] = total
    most = jnp.maximum(jnp.maximum(a[128:], b[128:]), jnp.maximum(c[128:], d[128:]))
    most_ref[0] = jnp.max(most).astype(I32)
    for g in range(CLASSES):
        out_ref[:, g * LANES : (g + 1) * LANES] = jnp.where(cls == g, total, 0.0).astype(BF16)


def params(mib):
    return pltpu.CompilerParams(vmem_limit_bytes=mib << 20)


def cost(flops, nbytes):
    return pl.CostEstimate(flops=flops, bytes_accessed=nbytes, transcendentals=0)


def shift(a, axis, size, k):
    return lax.ppermute(a, axis, [(i, (i + k) % size) for i in range(size)])


def one_round(start, prev, amplitudes, integrals, occ_irrep, vir_irrep, cd_list):
    n_occ, n_vir = occ_irrep.shape[0], vir_irrep.shape[0]
    rows, pairs = amplitudes.shape
    cols = integrals.shape[1]
    sds = jax.ShapeDtypeStruct
    occ = occ_irrep.reshape(1, n_occ)
    packed, hot, symt, most = pl.pallas_call(
        functools.partial(pack_kernel, n_occ, n_vir),
        out_shape=(
            sds((rows, SLOTS), BF16),
            sds((SLOTS, pairs), BF16),
            sds((LANES, LANES), F32),
            sds((8, LANES), F32),
        ),
        in_specs=[SMEM, VMEM, VMEM, VMEM, VMEM],
        out_specs=(VMEM,) * 4,
        scratch_shapes=[
            pltpu.VMEM((1, LANES), I32),
            pltpu.VMEM((1, 10 * LANES), I32),
            pltpu.VMEM((2 * pairs // LANES, LANES), I32),
        ],
        compiler_params=params(8),
        cost_estimate=cost(2 * rows * pairs * SLOTS, 6 << 20),
        name="pack",
    )(start, occ, vir_irrep.reshape(1, n_vir), cd_list, amplitudes)

    parts = []
    width = 256
    for part in range(cols // width):
        parts.append(
            pl.pallas_call(
                functools.partial(weights_kernel, part),
                out_shape=sds((SLOTS, width), BF16),
                grid=(1,),
                in_specs=[VMEM, VMEM, pl.BlockSpec((pairs, width), lambda i, part=part: (0, part))],
                out_specs=VMEM,
                scratch_shapes=[pltpu.VMEM((pairs, width), BF16)],
                compiler_params=params(16),
                cost_estimate=cost(2 * width * pairs * SLOTS, 7 << 20),
                name="weights",
            )(hot, symt, integrals)
        )

    near = [packed]
    order = [0]
    for k in (1, 3, 2):
        near.append(shift(packed, "x", 4, k))
        order.append(4 - k)
    mine = jnp.concatenate(near, axis=0)
    blocks, places = [mine], [(0, order)]
    up = down = mine
    for k in range(1, 5):
        up = shift(up, "z", 8, 1)
        blocks.append(up)
        places.append((8 - k, order))
        if k < 4:
            down = shift(down, "z", 8, 7)
            blocks.append(down)
            places.append((k, order))

    keep, send = pl.pallas_call(
        functools.partial(product_kernel, n_occ, places),
        out_shape=(sds((4, 136, LANES), F32),) * 2,
        in_specs=[VMEM] * (2 + len(blocks) + len(parts)),
        out_specs=(VMEM,) * 2,
        scratch_shapes=[
            pltpu.VMEM((1024, SLOTS), BF16),
            pltpu.VMEM((8, 128, LANES), F32),
            pltpu.VMEM((1, LANES), I32),
        ],
        compiler_params=params(16),
        cost_estimate=cost(2 * 1024 * cols * SLOTS, 4 << 20),
        name="product",
    )(occ, most, *blocks, *parts)

    got = shift(send, "core", 2, 1)
    folded = pl.pallas_call(
        fold_kernel,
        out_shape=(sds((136, LANES), F32),) * 4,
        in_specs=[VMEM] * 2,
        out_specs=(VMEM,) * 4,
        compiler_params=params(8),
        name="fold",
    )(keep, got)
    arrived = [folded[0]] + [shift(folded[k], "y", 4, k) for k in (2, 1, 3)]
    kernel = functools.partial(finish_kernel, n_occ)
    if prev is None:
        kernel = lambda occ_ref, *refs: finish_kernel(n_occ, occ_ref, None, *refs)
    extra = () if prev is None else (prev,)
    return pl.pallas_call(
        kernel,
        out_shape=(sds((128, cols), BF16), sds((128, LANES), F32), sds((1,), I32)),
        in_specs=[VMEM] * (5 + len(extra)),
        out_specs=(VMEM, VMEM, SMEM),
        scratch_shapes=[pltpu.VMEM((1, LANES), I32)],
        compiler_params=params(8),
        name="finish",
    )(occ, *extra, *arrived)


def local(amplitudes, integrals, occ_irrep, vir_irrep, cd_list, ab_list):
    args = (amplitudes, integrals, occ_irrep, vir_irrep, cd_list)
    out, total, most = one_round(jnp.zeros((1,), I32), None, *args)

    def more(out, total, most):
        def body(state):
            k, _, total = state
            out, total, _ = one_round((k * SLOTS).reshape(1), total, *args)
            return k + 1, out, total

        return lax.while_loop(lambda s: s[0] * SLOTS < most[0], body, (jnp.int32(1), out, total))[1]

    return lax.cond(most[0] > SLOTS, more, lambda out, total, most: out, out, total, most)


def solution(mesh):
    fine = Mesh(mesh.devices.reshape(4, 2, 8, 4), ("y", "core", "z", "x"))
    owner, group = ("y", "core"), ("z", "x")
    return jax.shard_map(
        local,
        mesh=fine,
        in_specs=(P(group, owner), P(owner, group), P(), P(), P(None, owner), P(None, group)),
        out_specs=P(owner, group),
        check_vma=False,
    )
```

```python
import functools

import jax
import jax.numpy as jnp
from jax import lax
from jax.experimental import pallas as pl
from jax.experimental.pallas import tpu as pltpu
from jax.sharding import Mesh, PartitionSpec as P


LANES = 128
CLASSES = 8
SLOTS = 640
CHUNK, WINDOW = 1024, 256
F32, BF16, I32 = jnp.float32, jnp.bfloat16, jnp.int32
VMEM = pl.BlockSpec(memory_space=pltpu.VMEM)
SMEM = pl.BlockSpec(memory_space=pltpu.SMEM)
ANY = pl.BlockSpec(memory_space=pl.ANY)
WIDTH = 256


def iota(shape, dim):
    return lax.broadcasted_iota(I32, shape, dim)


def row_classes(occ_row, first, rows, n_occ):
    r = first + iota((rows, LANES), 0)
    i = jnp.zeros_like(r)
    for m in range(1, 11):
        i = i + (r >= m * n_occ).astype(I32)
    j = r - i * n_occ
    lane = iota((rows, LANES), 1)
    occ = jnp.broadcast_to(occ_row, (rows, LANES))
    a = jnp.sum(jnp.where(lane == i, occ, 0), axis=1, keepdims=True)
    b = jnp.sum(jnp.where(lane == j, occ, 0), axis=1, keepdims=True)
    return jnp.bitwise_xor(a, b)


def pack_kernel(
    n_occ, n_vir, start, occ_ref, vir_ref, cd_ref, amp_ref, w_ref,
    t_ref, hot_ref, slot_ref, symt_ref, cnt_ref, win_ref, next_ref, occ_s, vir_s, idx_s, acc, kept, sem
):
    load = quarter(w_ref, next_ref, 0, sem)
    rows, pairs = amp_ref.shape
    chunks = pairs // LANES
    occ_s[...] = jnp.zeros_like(occ_s)
    occ_s[:, :n_occ] = occ_ref[...]
    vir_s[...] = jnp.zeros_like(vir_s)
    vir_s[:, :n_vir] = vir_ref[...].reshape(1, n_vir)
    for m in range(chunks):
        for k in range(2):
            idx_s[k * chunks + m : k * chunks + m + 1, :] = cd_ref[k : k + 1, m * LANES : (m + 1) * LANES]
    words = []
    for w in range(2):
        word = jnp.zeros((1, LANES), I32)
        for k in range(8):
            at = (w * 8 + k) * LANES
            if at < n_vir:
                word = word | (vir_s[:, at : at + LANES] << (4 * k))
        words.append(word)
    idx = idx_s[...]
    low, high = idx & (LANES - 1), idx >> 7
    found = [
        jnp.take_along_axis(jnp.broadcast_to(w, idx.shape), low, axis=1, mode="promise_in_bounds") for w in words
    ]
    label = lax.shift_right_logical(jnp.where(high < 8, found[0], found[1]), (high & 7) * 4) & 7
    sym = jnp.bitwise_xor(label[:chunks], label[chunks:])

    hot = jnp.concatenate([(sym == g).astype(F32) for g in range(CLASSES)], axis=0).astype(BF16)
    before = (iota((LANES, LANES), 0) < iota((LANES, LANES), 1)).astype(F32).astype(BF16)
    inside = jnp.dot(hot, before, preferred_element_type=F32)
    total = jnp.dot(hot, jnp.ones((LANES, LANES), BF16), preferred_element_type=F32)
    earlier = (iota((chunks, chunks), 1) < iota((chunks, chunks), 0)).astype(F32).astype(BF16)
    slot = jnp.zeros((chunks, LANES), F32)
    first = jnp.full((chunks, LANES), 2.0 * pairs, F32)
    last = jnp.zeros((chunks, LANES), F32)
    for g in range(CLASSES):
        part = slice(g * chunks, (g + 1) * chunks)
        base = jnp.dot(earlier, total[part].astype(BF16), preferred_element_type=F32)
        slot = jnp.where(sym == g, inside[part] + base, slot)
        first = jnp.minimum(first, base)
        last = jnp.maximum(last, base + total[part])
    cnt_ref[...] = jnp.broadcast_to(last[chunks - 1 :, :], cnt_ref.shape)
    slot = slot.astype(I32) - start[0]
    slot_ref[...] = slot
    wide = jnp.concatenate([sym, jnp.zeros((LANES - chunks, LANES), I32)], axis=0).astype(F32)
    symt_ref[...] = wide.T

    gidx = lax.axis_index("z") * 4 + lax.axis_index("x")
    cls = row_classes(occ_s[...], gidx * rows, rows, n_occ)
    acc[...] = jnp.zeros_like(acc)
    per = CHUNK // LANES

    def place(kept, one, low):
        out = lax.dot_general(kept, one, (((1,), (1,)), ((), ())), preferred_element_type=F32)
        out = jnp.concatenate([out, jnp.zeros((rows, LANES), F32)], axis=1)
        at = pl.ds(pl.multiple_of(low // LANES * LANES, LANES), WINDOW + LANES)
        acc[:, at] += pltpu.roll(out, lax.rem(low, LANES), axis=1)

    lows = []
    for c in range(pairs // CHUNK):
        low = jnp.max(first[c * per : c * per + 1]).astype(I32) - start[0]
        high = jnp.max(last[(c + 1) * per - 1 : (c + 1) * per]).astype(I32) - start[0]
        low = jnp.clip(low, 0, SLOTS - 16) // 16 * 16
        lows.append((low, (jnp.minimum(high, SLOTS) - low + WINDOW - 1) // WINDOW))
    for c, (low, windows) in enumerate(lows):
        win_ref[2 * c] = low
        win_ref[2 * c + 1] = windows
        amp = amp_ref[:, c * CHUNK : (c + 1) * CHUNK].astype(F32)
        kept[:, c * CHUNK : (c + 1) * CHUNK] = jnp.where(cls == lines(sym, c, per), amp, 0.0).astype(BF16)
        one = one_hot(lines(slot, c, per), low)
        hot_ref[c] = one
        place(kept[:, c * CHUNK : (c + 1) * CHUNK], one, low)
    for c, (low, windows) in enumerate(lows):

        @pl.loop(1, windows)
        def _(i):
            at = low + i * WINDOW
            place(kept[:, c * CHUNK : (c + 1) * CHUNK], one_hot(lines(slot_ref[...], c, per), at), at)

    t_ref[...] = acc[:, :SLOTS].astype(BF16)
    load.wait()


def lines(a, c, per):
    return jnp.concatenate([a[c * per + i : c * per + i + 1] for i in range(per)], axis=1)


def one_hot(line, low):
    return (iota((WINDOW, CHUNK), 0) == line - low).astype(F32).astype(BF16)


def quarter(w_ref, into, part, sem):
    copy = pltpu.make_async_copy(w_ref.at[:, part * WIDTH : (part + 1) * WIDTH], into, sem)
    copy.start()
    return copy


def weights_kernel(part, more, win, hot_ref, slot_ref, symt_ref, ready_ref, *refs):
    if more:
        w_ref, out_ref, next_ref, kept, acc, sem = refs
        load = quarter(w_ref, next_ref, part + 1, sem)
    else:
        out_ref, kept, acc = refs
    width = out_ref.shape[1]
    per = CHUNK // LANES
    acc[...] = jnp.zeros_like(acc)
    for c in range(ready_ref.shape[0] // CHUNK):
        for m in range(per):
            sym = jnp.broadcast_to(symt_ref[:, c * per + m : c * per + m + 1], (LANES, LANES)).astype(BF16)
            rows = slice(c * CHUNK + m * LANES, c * CHUNK + (m + 1) * LANES)
            for q in range(width // LANES):
                g = part * (width // LANES) + q
                w = ready_ref[rows, q * LANES : (q + 1) * LANES]
                kept[m * LANES : (m + 1) * LANES, q * LANES : (q + 1) * LANES] = jnp.where(sym == BF16(g), w, BF16(0))
        low = win[2 * c]
        at = pl.ds(pl.multiple_of(low, 16), WINDOW)
        acc[at, :] += jnp.dot(hot_ref[c], kept[...], preferred_element_type=F32)

        @pl.loop(1, win[2 * c + 1])
        def _(i):
            at = pl.multiple_of(low + i * WINDOW, 16)
            one = one_hot(lines(slot_ref[...], c, per), at)
            acc[pl.ds(at, WINDOW), :] += jnp.dot(one, kept[...], preferred_element_type=F32)

    out_ref[...] = acc[:SLOTS].astype(BF16)
    if more:
        load.wait()


def multiply(n_occ, places, occ_ref, blocks, weights, out, occ_s):
    z, x = lax.axis_index("z"), lax.axis_index("x")
    occ_s[...] = jnp.zeros_like(occ_s)
    occ_s[:, :n_occ] = occ_ref[...]
    for ref, (dz, order) in zip(blocks, places):
        height = ref.shape[0]
        owner = (z + dz) % 8
        total = jnp.zeros((height, LANES), F32)
        piece = height // len(order)
        starts = [owner * height + (x + dx) % 4 * piece for dx in order]
        cls = jnp.concatenate([row_classes(occ_s[...], at, piece, n_occ) for at in starts], axis=0)
        for p, w in enumerate(weights):
            part = jnp.dot(ref[...], w[...], preferred_element_type=F32)
            for q in range(w.shape[1] // LANES):
                g = p * (w.shape[1] // LANES) + q
                total = total + jnp.where(cls == g, part[:, q * LANES : (q + 1) * LANES], 0.0)
        for j, dx in enumerate(order):
            at = pl.ds(pl.multiple_of((x + dx) % 4 * piece, piece), piece)
            out[owner, at] = total[j * piece : (j + 1) * piece]


def early_kernel(n_occ, places, occ_ref, *refs):
    n = len(places)
    sums_ref, occ_s = refs[-2:]
    multiply(n_occ, places, occ_ref, refs[:n], refs[n:-2], sums_ref, occ_s)


def product_kernel(n_occ, places, occ_ref, cnt_ref, early_ref, *refs):
    n = len(places)
    keep_ref, send_ref, sums_s, occ_s = refs[-4:]
    multiply(n_occ, places, occ_ref, refs[:n], refs[n:-4], sums_s, occ_s)
    core, z = lax.axis_index("core"), lax.axis_index("z")
    late = (z + places[0][0]) % 8
    for ref, odd in ((keep_ref, core), (send_ref, 1 - core)):
        for k in range(4):
            owner = 2 * k + odd

            @pl.when(owner != late)
            def _():
                ref[k, :128] = early_ref[owner]

            @pl.when(owner == late)
            def _():
                ref[k, :128] = sums_s[owner]

            ref[k, 128:] = cnt_ref[...]


def fold_kernel(keep_ref, got_ref, *outs):
    y = lax.axis_index("y")
    for k, out in enumerate(outs):
        at = (y + k) % 4
        out[:128] = keep_ref[at, :128] + got_ref[at, :128]
        out[128:] = jnp.maximum(keep_ref[at, 128:], got_ref[at, 128:])


def finish_kernel(n_occ, occ_ref, prev_ref, a, b, c, d, out_ref, sum_ref, most_ref, occ_s):
    first = (lax.axis_index("y") * 2 + lax.axis_index("core")) * 128
    occ_s[...] = jnp.zeros_like(occ_s)
    occ_s[:, :n_occ] = occ_ref[...]
    cls = row_classes(occ_s[...], first, 128, n_occ)
    total = (a[:128] + b[:128]) + (c[:128] + d[:128])
    if prev_ref is not None:
        total = total + prev_ref[...]
    sum_ref[...] = total
    most = jnp.maximum(jnp.maximum(a[128:], b[128:]), jnp.maximum(c[128:], d[128:]))
    most_ref[0] = jnp.max(most).astype(I32)
    for g in range(CLASSES):
        out_ref[:, g * LANES : (g + 1) * LANES] = jnp.where(cls == g, total, 0.0).astype(BF16)


def params(mib):
    return pltpu.CompilerParams(vmem_limit_bytes=mib << 20)


def cost(flops, nbytes):
    return pl.CostEstimate(flops=flops, bytes_accessed=nbytes, transcendentals=0)


def shift(a, axis, size, k):
    return lax.ppermute(a, axis, [(i, (i + k) % size) for i in range(size)])


def round_body(start, prev, amplitudes, integrals, occ_irrep, vir_irrep, cd_list):
    n_occ, n_vir = occ_irrep.shape[0], vir_irrep.shape[0]
    rows, pairs = amplitudes.shape
    cols = integrals.shape[1]
    sds = jax.ShapeDtypeStruct
    occ = occ_irrep.reshape(1, n_occ)
    packed, hot, slot, symt, most, win, ready = pl.pallas_call(
        functools.partial(pack_kernel, n_occ, n_vir),
        out_shape=(
            sds((rows, SLOTS), BF16),
            sds((pairs // CHUNK, WINDOW, CHUNK), BF16),
            sds((pairs // LANES, LANES), I32),
            sds((LANES, LANES), F32),
            sds((8, LANES), F32),
            sds((2 * pairs // CHUNK,), I32),
            pltpu.VMEM((pairs, WIDTH), BF16),
        ),
        in_specs=[SMEM, VMEM, VMEM, VMEM, VMEM, ANY],
        out_specs=(VMEM,) * 5 + (SMEM, VMEM),
        scratch_shapes=[
            pltpu.VMEM((1, LANES), I32),
            pltpu.VMEM((1, 10 * LANES), I32),
            pltpu.VMEM((2 * pairs // LANES, LANES), I32),
            pltpu.VMEM((rows, SLOTS + 3 * LANES), F32),
            pltpu.VMEM((rows, pairs), BF16),
            pltpu.SemaphoreType.DMA,
        ],
        compiler_params=params(8),
        cost_estimate=cost(2 * rows * pairs * SLOTS, 6 << 20),
        name="pack",
    )(start, occ, vir_irrep, cd_list, amplitudes, integrals)

    parts = []
    count = cols // WIDTH
    for k in range(count):
        more = k + 1 < count
        out = (sds((SLOTS, WIDTH), BF16),) + more * (pltpu.VMEM((pairs, WIDTH), BF16),)
        scratch = [pltpu.VMEM((CHUNK, WIDTH), BF16), pltpu.VMEM((SLOTS + WINDOW, WIDTH), F32)]
        part, *ready = pl.pallas_call(
            functools.partial(weights_kernel, k, more),
            out_shape=out,
            in_specs=[SMEM, VMEM, VMEM, VMEM, VMEM] + more * [ANY],
            out_specs=(VMEM,) * len(out),
            scratch_shapes=scratch + more * [pltpu.SemaphoreType.DMA],
            compiler_params=params(16),
            cost_estimate=cost(2 * WIDTH * pairs * SLOTS, 7 << 20),
            name="weights",
        )(win, hot, slot, symt, ready, *(more * (integrals,)))
        parts.append(part)
        ready = ready[0] if more else None

    near = [packed] + [shift(packed, "x", 4, k) for k in (2, 1, 3)]
    order = (0, 2, 3, 1)
    mine = jnp.concatenate(near, axis=0)
    blocks, places = [mine], [(0, order)]
    up = down = mine
    for k in range(1, 5):
        up = shift(up, "z", 8, 1)
        blocks.append(up)
        places.append((8 - k, order))
        if k < 4:
            down = shift(down, "z", 8, 7)
            blocks.append(down)
            places.append((k, order))

    sums = sds((8, 128, LANES), F32)
    early = pl.pallas_call(
        functools.partial(early_kernel, n_occ, places[:-1]),
        out_shape=sums,
        in_specs=[VMEM] * (len(blocks) + len(parts)),
        out_specs=VMEM,
        scratch_shapes=[pltpu.VMEM((1, LANES), I32)],
        compiler_params=params(8),
        cost_estimate=cost(2 * 896 * cols * SLOTS, 4 << 20),
        name="early",
    )(occ, *blocks[:-1], *parts)
    keep, send = pl.pallas_call(
        functools.partial(product_kernel, n_occ, places[-1:]),
        out_shape=(sds((4, 136, LANES), F32),) * 2,
        in_specs=[VMEM] * (4 + len(parts)),
        out_specs=(VMEM,) * 2,
        scratch_shapes=[pltpu.VMEM((8, 128, LANES), F32), pltpu.VMEM((1, LANES), I32)],
        compiler_params=params(8),
        cost_estimate=cost(2 * 128 * cols * SLOTS, 1 << 20),
        name="product",
    )(occ, most, early, blocks[-1], *parts)

    got = shift(send, "core", 2, 1)
    folded = pl.pallas_call(
        fold_kernel,
        out_shape=(sds((136, LANES), F32),) * 4,
        in_specs=[VMEM] * 2,
        out_specs=(VMEM,) * 4,
        compiler_params=params(8),
        name="fold",
    )(keep, got)
    arrived = [folded[0]] + [shift(folded[k], "y", 4, k) for k in (2, 1, 3)]
    kernel = functools.partial(finish_kernel, n_occ)
    if prev is None:
        kernel = lambda occ_ref, *refs: finish_kernel(n_occ, occ_ref, None, *refs)
    extra = () if prev is None else (prev,)
    return pl.pallas_call(
        kernel,
        out_shape=(sds((128, cols), BF16), sds((128, LANES), F32), sds((1,), I32)),
        in_specs=[VMEM] * (5 + len(extra)),
        out_specs=(VMEM, VMEM, SMEM),
        scratch_shapes=[pltpu.VMEM((1, LANES), I32)],
        compiler_params=params(8),
        name="finish",
    )(occ, *extra, *arrived)


def local(amplitudes, integrals, occ_irrep, vir_irrep, cd_list, ab_list):
    args = (amplitudes, integrals, occ_irrep, vir_irrep, cd_list)
    out, total, most = round_body(jnp.zeros((1,), I32), None, *args)

    def more(out, total, most):
        def body(state):
            k, _, total = state
            out, total, _ = round_body((k * SLOTS).reshape(1), total, *args)
            return k + 1, out, total

        return lax.while_loop(lambda s: s[0] * SLOTS < most[0], body, (jnp.int32(1), out, total))[1]

    return lax.cond(most[0] > SLOTS, more, lambda out, total, most: out, out, total, most)


def solution(mesh):
    fine = Mesh(mesh.devices.reshape(4, 2, 8, 4), ("y", "core", "z", "x"))
    owner, group = ("y", "core"), ("z", "x")
    return jax.shard_map(
        local,
        mesh=fine,
        in_specs=(P(group, owner), P(owner, group), P(), P(), P(None, owner), P(None, group)),
        out_specs=P(owner, group),
        check_vma=False,
    )
```

```python
import functools

import jax
import jax.numpy as jnp
from jax import lax
from jax.experimental import pallas as pl
from jax.experimental.pallas import tpu as pltpu
from jax.sharding import Mesh, PartitionSpec as P


LANES = 128
CLASSES = 8
SLOTS = 640
CHUNK, WINDOW = 1024, 256
F32, BF16, I32 = jnp.float32, jnp.bfloat16, jnp.int32
VMEM = pl.BlockSpec(memory_space=pltpu.VMEM)
SMEM = pl.BlockSpec(memory_space=pltpu.SMEM)
ANY = pl.BlockSpec(memory_space=pl.ANY)
WIDTH = 256


def iota(shape, dim):
    return lax.broadcasted_iota(I32, shape, dim)


def row_classes(occ_row, first, rows, n_occ):
    r = first + iota((rows, LANES), 0)
    i = jnp.zeros_like(r)
    for m in range(1, 11):
        i = i + (r >= m * n_occ).astype(I32)
    j = r - i * n_occ
    lane = iota((rows, LANES), 1)
    occ = jnp.broadcast_to(occ_row, (rows, LANES))
    a = jnp.sum(jnp.where(lane == i, occ, 0), axis=1, keepdims=True)
    b = jnp.sum(jnp.where(lane == j, occ, 0), axis=1, keepdims=True)
    return jnp.bitwise_xor(a, b)


def pack_kernel(
    n_occ, n_vir, start, occ_ref, vir_ref, cd_ref, amp_ref,
    t_ref, hot_ref, slot_ref, symt_ref, cnt_ref, win_ref, occ_s, vir_s, idx_s, acc, kept
):
    rows, pairs = amp_ref.shape
    chunks = pairs // LANES
    occ_s[...] = jnp.zeros_like(occ_s)
    occ_s[:, :n_occ] = occ_ref[...]
    vir_s[...] = jnp.zeros_like(vir_s)
    vir_s[:, :n_vir] = vir_ref[...].reshape(1, n_vir)
    for m in range(chunks):
        for k in range(2):
            idx_s[k * chunks + m : k * chunks + m + 1, :] = cd_ref[k : k + 1, m * LANES : (m + 1) * LANES]
    words = []
    for w in range(2):
        word = jnp.zeros((1, LANES), I32)
        for k in range(8):
            at = (w * 8 + k) * LANES
            if at < n_vir:
                word = word | (vir_s[:, at : at + LANES] << (4 * k))
        words.append(word)
    idx = idx_s[...]
    low, high = idx & (LANES - 1), idx >> 7
    found = [
        jnp.take_along_axis(jnp.broadcast_to(w, idx.shape), low, axis=1, mode="promise_in_bounds") for w in words
    ]
    label = lax.shift_right_logical(jnp.where(high < 8, found[0], found[1]), (high & 7) * 4) & 7
    sym = jnp.bitwise_xor(label[:chunks], label[chunks:])

    hot = jnp.concatenate([(sym == g).astype(F32) for g in range(CLASSES)], axis=0).astype(BF16)
    before = (iota((LANES, LANES), 0) < iota((LANES, LANES), 1)).astype(F32).astype(BF16)
    inside = jnp.dot(hot, before, preferred_element_type=F32)
    total = jnp.dot(hot, jnp.ones((LANES, LANES), BF16), preferred_element_type=F32)
    earlier = (iota((chunks, chunks), 1) < iota((chunks, chunks), 0)).astype(F32).astype(BF16)
    slot = jnp.zeros((chunks, LANES), F32)
    first = jnp.full((chunks, LANES), 2.0 * pairs, F32)
    last = jnp.zeros((chunks, LANES), F32)
    for g in range(CLASSES):
        part = slice(g * chunks, (g + 1) * chunks)
        base = jnp.dot(earlier, total[part].astype(BF16), preferred_element_type=F32)
        slot = jnp.where(sym == g, inside[part] + base, slot)
        first = jnp.minimum(first, base)
        last = jnp.maximum(last, base + total[part])
    cnt_ref[...] = jnp.broadcast_to(last[chunks - 1 :, :], cnt_ref.shape)
    slot = slot.astype(I32) - start[0]
    slot_ref[...] = slot
    wide = jnp.concatenate([sym, jnp.zeros((LANES - chunks, LANES), I32)], axis=0).astype(F32)
    symt_ref[...] = wide.T

    gidx = lax.axis_index("z") * 4 + lax.axis_index("x")
    cls = row_classes(occ_s[...], gidx * rows, rows, n_occ)
    acc[...] = jnp.zeros_like(acc)
    per = CHUNK // LANES

    def place(kept, one, low):
        out = lax.dot_general(kept, one, (((1,), (1,)), ((), ())), preferred_element_type=F32)
        out = jnp.concatenate([out, jnp.zeros((rows, LANES), F32)], axis=1)
        at = pl.ds(pl.multiple_of(low // LANES * LANES, LANES), WINDOW + LANES)
        acc[:, at] += pltpu.roll(out, lax.rem(low, LANES), axis=1)

    lows = []
    for c in range(pairs // CHUNK):
        low = jnp.max(first[c * per : c * per + 1]).astype(I32) - start[0]
        high = jnp.max(last[(c + 1) * per - 1 : (c + 1) * per]).astype(I32) - start[0]
        low = jnp.clip(low, 0, SLOTS - 16) // 16 * 16
        lows.append((low, (jnp.minimum(high, SLOTS) - low + WINDOW - 1) // WINDOW))
    for c, (low, windows) in enumerate(lows):
        win_ref[2 * c] = low
        win_ref[2 * c + 1] = windows
        amp = amp_ref[:, c * CHUNK : (c + 1) * CHUNK].astype(F32)
        kept[:, c * CHUNK : (c + 1) * CHUNK] = jnp.where(cls == lines(sym, c, per), amp, 0.0).astype(BF16)
        one = one_hot(lines(slot, c, per), low)
        hot_ref[c] = one
        place(kept[:, c * CHUNK : (c + 1) * CHUNK], one, low)
    for c, (low, windows) in enumerate(lows):

        @pl.loop(1, windows)
        def _(i):
            at = low + i * WINDOW
            place(kept[:, c * CHUNK : (c + 1) * CHUNK], one_hot(lines(slot_ref[...], c, per), at), at)

    t_ref[...] = acc[:, :SLOTS].astype(BF16)


def lines(a, c, per):
    return jnp.concatenate([a[c * per + i : c * per + i + 1] for i in range(per)], axis=1)


def one_hot(line, low):
    return (iota((WINDOW, CHUNK), 0) == line - low).astype(F32).astype(BF16)


def quarter(w_ref, into, part, sem):
    copy = pltpu.make_async_copy(w_ref.at[:, part * WIDTH : (part + 1) * WIDTH], into, sem)
    copy.start()
    return copy


def first_weights_kernel(win, hot_ref, slot_ref, symt_ref, w_ref, out_ref, next_ref, kept, acc, raw, sems, sem):
    copies = []
    for c in range(w_ref.shape[0] // CHUNK):
        rows = slice(c * CHUNK, (c + 1) * CHUNK)
        copies.append(pltpu.make_async_copy(w_ref.at[rows, :WIDTH], raw.at[rows], sems.at[c]))
        copies[-1].start()
    load = quarter(w_ref, next_ref, 1, sem)
    pack_weights(0, win, hot_ref, slot_ref, symt_ref, raw, out_ref, kept, acc, copies)
    load.wait()


def weights_kernel(part, more, win, hot_ref, slot_ref, symt_ref, ready_ref, *refs):
    if more:
        w_ref, out_ref, next_ref, kept, acc, sem = refs
        load = quarter(w_ref, next_ref, part + 1, sem)
    else:
        out_ref, kept, acc = refs
    pack_weights(part, win, hot_ref, slot_ref, symt_ref, ready_ref, out_ref, kept, acc)
    if more:
        load.wait()


def pack_weights(part, win, hot_ref, slot_ref, symt_ref, ready_ref, out_ref, kept, acc, copies=None):
    width = out_ref.shape[1]
    per = CHUNK // LANES
    acc[...] = jnp.zeros_like(acc)
    for c in range(ready_ref.shape[0] // CHUNK):
        if copies:
            copies[c].wait()
        for m in range(per):
            sym = jnp.broadcast_to(symt_ref[:, c * per + m : c * per + m + 1], (LANES, LANES)).astype(BF16)
            rows = slice(c * CHUNK + m * LANES, c * CHUNK + (m + 1) * LANES)
            for q in range(width // LANES):
                g = part * (width // LANES) + q
                w = ready_ref[rows, q * LANES : (q + 1) * LANES]
                kept[m * LANES : (m + 1) * LANES, q * LANES : (q + 1) * LANES] = jnp.where(sym == BF16(g), w, BF16(0))
        low = win[2 * c]
        at = pl.ds(pl.multiple_of(low, 16), WINDOW)
        acc[at, :] += jnp.dot(hot_ref[c], kept[...], preferred_element_type=F32)

        @pl.loop(1, win[2 * c + 1])
        def _(i):
            at = pl.multiple_of(low + i * WINDOW, 16)
            one = one_hot(lines(slot_ref[...], c, per), at)
            acc[pl.ds(at, WINDOW), :] += jnp.dot(one, kept[...], preferred_element_type=F32)

    out_ref[...] = acc[:SLOTS].astype(BF16)


def multiply(n_occ, places, occ_ref, blocks, weights, out, occ_s):
    z, x = lax.axis_index("z"), lax.axis_index("x")
    sign = 2 * (z % 2) - 1
    occ_s[...] = jnp.zeros_like(occ_s)
    occ_s[:, :n_occ] = occ_ref[...]
    for ref, (dz, order) in zip(blocks, places):
        height = ref.shape[0]
        owner = (z + dz * sign + 8) % 8
        total = jnp.zeros((height, LANES), F32)
        piece = height // len(order)
        starts = [owner * height + jnp.bitwise_xor(x, dx) * piece for dx in order]
        cls = jnp.concatenate([row_classes(occ_s[...], at, piece, n_occ) for at in starts], axis=0)
        for p, w in enumerate(weights):
            part = jnp.dot(ref[...], w[...], preferred_element_type=F32)
            for q in range(w.shape[1] // LANES):
                g = p * (w.shape[1] // LANES) + q
                total = total + jnp.where(cls == g, part[:, q * LANES : (q + 1) * LANES], 0.0)
        for j, dx in enumerate(order):
            at = pl.ds(pl.multiple_of(jnp.bitwise_xor(x, dx) * piece, piece), piece)
            out[owner, at] = total[j * piece : (j + 1) * piece]


def early_kernel(n_occ, places, occ_ref, *refs):
    n = len(places)
    sums_ref, occ_s = refs[-2:]
    multiply(n_occ, places, occ_ref, refs[:n], refs[n:-2], sums_ref, occ_s)


def product_kernel(n_occ, places, occ_ref, cnt_ref, early_ref, *refs):
    n = len(places)
    keep_ref, send_ref, sums_s, occ_s = refs[-4:]
    multiply(n_occ, places, occ_ref, refs[:n], refs[n:-4], sums_s, occ_s)
    core, z = lax.axis_index("core"), lax.axis_index("z")
    late = (z + 4) % 8
    for ref, odd in ((keep_ref, core), (send_ref, 1 - core)):
        for k in range(4):
            owner = 2 * k + odd

            @pl.when(owner != late)
            def _():
                ref[k, :128] = early_ref[owner]

            @pl.when(owner == late)
            def _():
                ref[k, :128] = sums_s[owner]

            ref[k, 128:] = cnt_ref[...]


def fold_kernel(order, keep_ref, got_ref, *outs):
    y = lax.axis_index("y")
    for k, out in zip(order, outs):
        at = jnp.bitwise_xor(y, k)
        out[:128] = keep_ref[at, :128] + got_ref[at, :128]
        out[128:] = jnp.maximum(keep_ref[at, 128:], got_ref[at, 128:])


def finish_kernel(n_occ, occ_ref, prev_ref, a, b, c, d, out_ref, sum_ref, most_ref, more_ref, occ_s):
    first = (lax.axis_index("y") * 2 + lax.axis_index("core")) * 128
    occ_s[...] = jnp.zeros_like(occ_s)
    occ_s[:, :n_occ] = occ_ref[...]
    cls = row_classes(occ_s[...], first, 128, n_occ)
    total = (a[:128] + b[:128]) + (c[:128] + d[:128])
    if prev_ref is not None:
        total = total + prev_ref[...]
    sum_ref[...] = total
    most = jnp.maximum(jnp.maximum(a[128:], b[128:]), jnp.maximum(c[128:], d[128:]))
    most_ref[0] = jnp.max(most).astype(I32)
    more_ref[0] = (most_ref[0] > SLOTS).astype(I32)
    for g in range(CLASSES):
        out_ref[:, g * LANES : (g + 1) * LANES] = jnp.where(cls == g, total, 0.0).astype(BF16)


def params(mib):
    return pltpu.CompilerParams(vmem_limit_bytes=mib << 20)


def cost(flops, nbytes):
    return pl.CostEstimate(flops=flops, bytes_accessed=nbytes, transcendentals=0)


def swap(a, axis, partner):
    pairs = [(i, partner(i)) for i in range(lax.axis_size(axis))]
    return lax.ppermute(a, axis, pairs)


def across(i):
    return (i + 1 if i % 2 else i + 7) % 8


def beside(i):
    return i ^ 1


def round_body(start, prev, amplitudes, integrals, occ_irrep, vir_irrep, cd_list):
    n_occ, n_vir = occ_irrep.shape[0], vir_irrep.shape[0]
    rows, pairs = amplitudes.shape
    cols = integrals.shape[1]
    sds = jax.ShapeDtypeStruct
    occ = occ_irrep.reshape(1, n_occ)
    packed, hot, slot, symt, most, win = pl.pallas_call(
        functools.partial(pack_kernel, n_occ, n_vir),
        out_shape=(
            sds((rows, SLOTS), BF16),
            sds((pairs // CHUNK, WINDOW, CHUNK), BF16),
            sds((pairs // LANES, LANES), I32),
            sds((LANES, LANES), F32),
            sds((8, LANES), F32),
            sds((2 * pairs // CHUNK,), I32),
        ),
        in_specs=[SMEM, VMEM, VMEM, VMEM, VMEM],
        out_specs=(VMEM,) * 5 + (SMEM,),
        scratch_shapes=[
            pltpu.VMEM((1, LANES), I32),
            pltpu.VMEM((1, 10 * LANES), I32),
            pltpu.VMEM((2 * pairs // LANES, LANES), I32),
            pltpu.VMEM((rows, SLOTS + 3 * LANES), F32),
            pltpu.VMEM((rows, pairs), BF16),
        ],
        compiler_params=params(8),
        cost_estimate=cost(2 * rows * pairs * SLOTS, 6 << 20),
        name="pack",
    )(start, occ, vir_irrep, cd_list, amplitudes)

    parts = []
    count = cols // WIDTH
    quarter_of = pltpu.VMEM((pairs, WIDTH), BF16)
    for k in range(count):
        more = k + 1 < count
        out = (sds((SLOTS, WIDTH), BF16),) + more * (quarter_of,)
        scratch = [pltpu.VMEM((CHUNK, WIDTH), BF16), pltpu.VMEM((SLOTS + WINDOW, WIDTH), F32)]
        if k == 0:
            kernel, given, specs = first_weights_kernel, (integrals,), [ANY]
            scratch += [quarter_of, pltpu.SemaphoreType.DMA((pairs // CHUNK,))]
        else:
            kernel, given, specs = functools.partial(weights_kernel, k, more), (ready, integrals), [VMEM, ANY]
        if not more:
            given, specs = given[:1], specs[:1]
        part, *ready = pl.pallas_call(
            kernel,
            out_shape=out,
            in_specs=[SMEM, VMEM, VMEM, VMEM] + specs,
            out_specs=(VMEM,) * len(out),
            scratch_shapes=scratch + more * [pltpu.SemaphoreType.DMA],
            compiler_params=params(16),
            cost_estimate=cost(2 * WIDTH * pairs * SLOTS, 7 << 20),
            name="weights",
        )(win, hot, slot, symt, *given)
        parts.append(part)
        ready = ready[0] if more else None

    order = (0, 2, 3, 1)
    near = [packed] + [swap(packed, "x", lambda i, m=m: i ^ m) for m in order[1:]]
    mine = jnp.concatenate(near, axis=0)
    blocks, places = [mine], [(0, order)]
    far, close = mine, mine
    for k in range(1, 4):
        far, close = swap(close, "z", across), swap(far, "z", beside)
        blocks += [far, close]
        places += [(k, order), (-k, order)]
    blocks.append(swap(far, "z", beside))
    places.append((4, order))

    sums = sds((8, 128, LANES), F32)
    early = pl.pallas_call(
        functools.partial(early_kernel, n_occ, places[:-1]),
        out_shape=sums,
        in_specs=[VMEM] * (len(blocks) + len(parts)),
        out_specs=VMEM,
        scratch_shapes=[pltpu.VMEM((1, LANES), I32)],
        compiler_params=params(8),
        cost_estimate=cost(2 * 896 * cols * SLOTS, 4 << 20),
        name="early",
    )(occ, *blocks[:-1], *parts)
    keep, send = pl.pallas_call(
        functools.partial(product_kernel, n_occ, places[-1:]),
        out_shape=(sds((4, 136, LANES), F32),) * 2,
        in_specs=[VMEM] * (4 + len(parts)),
        out_specs=(VMEM,) * 2,
        scratch_shapes=[pltpu.VMEM((8, 128, LANES), F32), pltpu.VMEM((1, LANES), I32)],
        compiler_params=params(8),
        cost_estimate=cost(2 * 128 * cols * SLOTS, 1 << 20),
        name="product",
    )(occ, most, early, blocks[-1], *parts)

    got = swap(send, "core", beside)
    folded = pl.pallas_call(
        functools.partial(fold_kernel, order),
        out_shape=(sds((136, LANES), F32),) * 4,
        in_specs=[VMEM] * 2,
        out_specs=(VMEM,) * 4,
        compiler_params=params(8),
        name="fold",
    )(keep, got)
    arrived = [folded[0]] + [swap(f, "y", lambda i, m=m: i ^ m) for m, f in zip(order[1:], folded[1:])]
    kernel = functools.partial(finish_kernel, n_occ)
    if prev is None:
        kernel = lambda occ_ref, *refs: finish_kernel(n_occ, occ_ref, None, *refs)
    extra = () if prev is None else (prev,)
    return pl.pallas_call(
        kernel,
        out_shape=(sds((128, cols), BF16), sds((128, LANES), F32), sds((1,), I32), sds((1,), I32)),
        in_specs=[VMEM] * (5 + len(extra)),
        out_specs=(VMEM, VMEM, SMEM, SMEM),
        scratch_shapes=[pltpu.VMEM((1, LANES), I32)],
        compiler_params=params(8),
        name="finish",
    )(occ, *extra, *arrived)


def local(amplitudes, integrals, occ_irrep, vir_irrep, cd_list, ab_list):
    args = (amplitudes, integrals, occ_irrep, vir_irrep, cd_list)
    out, total, most, more_rounds = round_body(jnp.zeros((1,), I32), None, *args)

    def more(out, total, most):
        def body(state):
            k, _, total = state
            out, total, _, _ = round_body((k * SLOTS).reshape(1), total, *args)
            return k + 1, out, total

        return lax.while_loop(lambda s: s[0] * SLOTS < most[0], body, (jnp.int32(1), out, total))[1]

    return lax.switch(more_rounds[0], (lambda out, total, most: out, more), out, total, most)


def solution(mesh):
    fine = Mesh(mesh.devices.reshape(4, 2, 8, 4), ("y", "core", "z", "x"))
    owner, group = ("y", "core"), ("z", "x")
    return jax.shard_map(
        local,
        mesh=fine,
        in_specs=(P(group, owner), P(owner, group), P(), P(), P(None, owner), P(None, group)),
        out_specs=P(owner, group),
        check_vma=False,
    )
```

```python
import functools

import jax
import jax.numpy as jnp
from jax import lax
from jax.experimental import pallas as pl
from jax.experimental.pallas import tpu as pltpu
from jax.sharding import Mesh, PartitionSpec as P


LANES = 128
CLASSES = 8
SLOTS = 640
CHUNK, WINDOW = 1024, 256
F32, BF16, I32 = jnp.float32, jnp.bfloat16, jnp.int32
VMEM = pl.BlockSpec(memory_space=pltpu.VMEM)
SMEM = pl.BlockSpec(memory_space=pltpu.SMEM)
ANY = pl.BlockSpec(memory_space=pl.ANY)
WIDTH = 256


def iota(shape, dim):
    return lax.broadcasted_iota(I32, shape, dim)


def row_classes(occ_row, first, rows, n_occ):
    r = first + iota((rows, LANES), 0)
    i = jnp.zeros_like(r)
    for m in range(1, 11):
        i = i + (r >= m * n_occ).astype(I32)
    j = r - i * n_occ
    lane = iota((rows, LANES), 1)
    occ = jnp.broadcast_to(occ_row, (rows, LANES))
    a = jnp.sum(jnp.where(lane == i, occ, 0), axis=1, keepdims=True)
    b = jnp.sum(jnp.where(lane == j, occ, 0), axis=1, keepdims=True)
    return jnp.bitwise_xor(a, b)


def pack_kernel(
    n_occ, n_vir, start, occ_ref, vir_ref, cd_ref, amp_ref,
    t_ref, hot_ref, slot_ref, symt_ref, cnt_ref, win_ref, occ_s, vir_s, idx_s, acc, kept
):
    rows, pairs = amp_ref.shape
    chunks = pairs // LANES
    occ_s[...] = jnp.zeros_like(occ_s)
    occ_s[:, :n_occ] = occ_ref[...]
    vir_s[...] = jnp.zeros_like(vir_s)
    vir_s[:, :n_vir] = vir_ref[...].reshape(1, n_vir)
    for m in range(chunks):
        for k in range(2):
            idx_s[k * chunks + m : k * chunks + m + 1, :] = cd_ref[k : k + 1, m * LANES : (m + 1) * LANES]
    words = []
    for w in range(2):
        word = jnp.zeros((1, LANES), I32)
        for k in range(8):
            at = (w * 8 + k) * LANES
            if at < n_vir:
                word = word | (vir_s[:, at : at + LANES] << (4 * k))
        words.append(word)
    idx = idx_s[...]
    low, high = idx & (LANES - 1), idx >> 7
    found = [
        jnp.take_along_axis(jnp.broadcast_to(w, idx.shape), low, axis=1, mode="promise_in_bounds") for w in words
    ]
    label = lax.shift_right_logical(jnp.where(high < 8, found[0], found[1]), (high & 7) * 4) & 7
    sym = jnp.bitwise_xor(label[:chunks], label[chunks:])

    hot = jnp.concatenate([(sym == g).astype(F32) for g in range(CLASSES)], axis=0).astype(BF16)
    before = (iota((LANES, LANES), 0) < iota((LANES, LANES), 1)).astype(F32).astype(BF16)
    inside = jnp.dot(hot, before, preferred_element_type=F32)
    total = jnp.dot(hot, jnp.ones((LANES, LANES), BF16), preferred_element_type=F32)
    earlier = (iota((chunks, chunks), 1) < iota((chunks, chunks), 0)).astype(F32).astype(BF16)
    slot = jnp.zeros((chunks, LANES), F32)
    first = jnp.full((chunks, LANES), 2.0 * pairs, F32)
    last = jnp.zeros((chunks, LANES), F32)
    for g in range(CLASSES):
        part = slice(g * chunks, (g + 1) * chunks)
        base = jnp.dot(earlier, total[part].astype(BF16), preferred_element_type=F32)
        slot = jnp.where(sym == g, inside[part] + base, slot)
        first = jnp.minimum(first, base)
        last = jnp.maximum(last, base + total[part])
    cnt_ref[...] = jnp.broadcast_to(last[chunks - 1 :, :], cnt_ref.shape)
    slot = slot.astype(I32) - start[0]
    slot_ref[...] = slot
    wide = jnp.concatenate([sym, jnp.zeros((LANES - chunks, LANES), I32)], axis=0).astype(F32)
    symt_ref[...] = wide.T

    gidx = lax.axis_index("z") * 4 + lax.axis_index("x")
    cls = row_classes(occ_s[...], gidx * rows, rows, n_occ)
    acc[...] = jnp.zeros_like(acc)
    per = CHUNK // LANES

    def place(kept, one, low):
        out = lax.dot_general(kept, one, (((1,), (1,)), ((), ())), preferred_element_type=F32)
        out = jnp.concatenate([out, jnp.zeros((rows, LANES), F32)], axis=1)
        at = pl.ds(pl.multiple_of(low // LANES * LANES, LANES), WINDOW + LANES)
        acc[:, at] += pltpu.roll(out, lax.rem(low, LANES), axis=1)

    lows = []
    for c in range(pairs // CHUNK):
        low = jnp.max(first[c * per : c * per + 1]).astype(I32) - start[0]
        high = jnp.max(last[(c + 1) * per - 1 : (c + 1) * per]).astype(I32) - start[0]
        low = jnp.clip(low, 0, SLOTS - 16) // 16 * 16
        lows.append((low, (jnp.minimum(high, SLOTS) - low + WINDOW - 1) // WINDOW))
    for c, (low, windows) in enumerate(lows):
        win_ref[2 * c] = low
        win_ref[2 * c + 1] = windows
        amp = amp_ref[:, c * CHUNK : (c + 1) * CHUNK].astype(F32)
        kept[:, c * CHUNK : (c + 1) * CHUNK] = jnp.where(cls == lines(sym, c, per), amp, 0.0).astype(BF16)
        one = one_hot(lines(slot, c, per), low)
        hot_ref[c] = one
        place(kept[:, c * CHUNK : (c + 1) * CHUNK], one, low)
    for c, (low, windows) in enumerate(lows):

        @pl.loop(1, windows)
        def _(i):
            at = low + i * WINDOW
            place(kept[:, c * CHUNK : (c + 1) * CHUNK], one_hot(lines(slot_ref[...], c, per), at), at)

    t_ref[...] = acc[:, :SLOTS].astype(BF16)


def lines(a, c, per):
    return jnp.concatenate([a[c * per + i : c * per + i + 1] for i in range(per)], axis=1)


def one_hot(line, low):
    return (iota((WINDOW, CHUNK), 0) == line - low).astype(F32).astype(BF16)


def quarter(w_ref, into, part, sem):
    copy = pltpu.make_async_copy(w_ref.at[:, part * WIDTH : (part + 1) * WIDTH], into, sem)
    copy.start()
    return copy


def first_weights_kernel(win, hot_ref, slot_ref, symt_ref, w_ref, out_ref, next_ref, kept, acc, raw, sems, sem):
    copies = []
    for c in range(w_ref.shape[0] // CHUNK):
        rows = slice(c * CHUNK, (c + 1) * CHUNK)
        copies.append(pltpu.make_async_copy(w_ref.at[rows, :WIDTH], raw.at[rows], sems.at[c]))
        copies[-1].start()
    load = quarter(w_ref, next_ref, 1, sem)
    pack_weights(0, win, hot_ref, slot_ref, symt_ref, raw, out_ref, kept, acc, copies)
    load.wait()


def weights_kernel(part, more, win, hot_ref, slot_ref, symt_ref, ready_ref, *refs):
    if more:
        w_ref, out_ref, next_ref, kept, acc, sem = refs
        load = quarter(w_ref, next_ref, part + 1, sem)
    else:
        out_ref, kept, acc = refs
    pack_weights(part, win, hot_ref, slot_ref, symt_ref, ready_ref, out_ref, kept, acc)
    if more:
        load.wait()


def pack_weights(part, win, hot_ref, slot_ref, symt_ref, ready_ref, out_ref, kept, acc, copies=None):
    width = out_ref.shape[1]
    per = CHUNK // LANES
    acc[...] = jnp.zeros_like(acc)
    for c in range(ready_ref.shape[0] // CHUNK):
        if copies:
            copies[c].wait()
        for m in range(per):
            sym = jnp.broadcast_to(symt_ref[:, c * per + m : c * per + m + 1], (LANES, LANES)).astype(BF16)
            rows = slice(c * CHUNK + m * LANES, c * CHUNK + (m + 1) * LANES)
            for q in range(width // LANES):
                g = part * (width // LANES) + q
                w = ready_ref[rows, q * LANES : (q + 1) * LANES]
                kept[m * LANES : (m + 1) * LANES, q * LANES : (q + 1) * LANES] = jnp.where(sym == BF16(g), w, BF16(0))
        low = win[2 * c]
        at = pl.ds(pl.multiple_of(low, 16), WINDOW)
        acc[at, :] += jnp.dot(hot_ref[c], kept[...], preferred_element_type=F32)

        @pl.loop(1, win[2 * c + 1])
        def _(i):
            at = pl.multiple_of(low + i * WINDOW, 16)
            one = one_hot(lines(slot_ref[...], c, per), at)
            acc[pl.ds(at, WINDOW), :] += jnp.dot(one, kept[...], preferred_element_type=F32)

    out_ref[...] = acc[:SLOTS].astype(BF16)


def multiply(n_occ, places, occ_ref, blocks, weights, out, occ_s):
    z, x = lax.axis_index("z"), lax.axis_index("x")
    sign = 2 * (z % 2) - 1
    occ_s[...] = jnp.zeros_like(occ_s)
    occ_s[:, :n_occ] = occ_ref[...]
    for ref, (dz, order) in zip(blocks, places):
        height = ref.shape[0]
        owner = (z + dz * sign + 8) % 8
        total = jnp.zeros((height, LANES), F32)
        piece = height // len(order)
        starts = [owner * height + jnp.bitwise_xor(x, dx) * piece for dx in order]
        cls = jnp.concatenate([row_classes(occ_s[...], at, piece, n_occ) for at in starts], axis=0)
        for p, w in enumerate(weights):
            part = jnp.dot(ref[...], w[...], preferred_element_type=F32)
            for q in range(w.shape[1] // LANES):
                g = p * (w.shape[1] // LANES) + q
                total = total + jnp.where(cls == g, part[:, q * LANES : (q + 1) * LANES], 0.0)
        for j, dx in enumerate(order):
            at = pl.ds(pl.multiple_of(jnp.bitwise_xor(x, dx) * piece, piece), piece)
            out[owner, at] = total[j * piece : (j + 1) * piece]


def early_kernel(n_occ, places, occ_ref, *refs):
    n = len(places)
    sums_ref, occ_s = refs[-2:]
    multiply(n_occ, places, occ_ref, refs[:n], refs[n:-2], sums_ref, occ_s)


def product_kernel(n_occ, places, occ_ref, cnt_ref, early_ref, *refs):
    n = len(places)
    keep_ref, send_ref, sums_s, occ_s = refs[-4:]
    multiply(n_occ, places, occ_ref, refs[:n], refs[n:-4], sums_s, occ_s)
    core, z = lax.axis_index("core"), lax.axis_index("z")
    sign = 2 * (z % 2) - 1
    late = [(z + dz * sign + 8) % 8 for dz, _ in places]
    for ref, odd in ((keep_ref, core), (send_ref, 1 - core)):
        for k in range(4):
            owner = 2 * k + odd

            is_late = functools.reduce(jnp.logical_or, [owner == at for at in late])

            @pl.when(jnp.logical_not(is_late))
            def _():
                ref[k, :128] = early_ref[owner]

            @pl.when(is_late)
            def _():
                ref[k, :128] = sums_s[owner]

            ref[k, 128:] = cnt_ref[...]


def fold_kernel(order, keep_ref, got_ref, *outs):
    y = lax.axis_index("y")
    for k, out in zip(order, outs):
        at = jnp.bitwise_xor(y, k)
        out[:128] = keep_ref[at, :128] + got_ref[at, :128]
        out[128:] = jnp.maximum(keep_ref[at, 128:], got_ref[at, 128:])


def finish_kernel(n_occ, occ_ref, prev_ref, a, b, c, d, out_ref, sum_ref, most_ref, more_ref, occ_s):
    first = (lax.axis_index("y") * 2 + lax.axis_index("core")) * 128
    occ_s[...] = jnp.zeros_like(occ_s)
    occ_s[:, :n_occ] = occ_ref[...]
    cls = row_classes(occ_s[...], first, 128, n_occ)
    total = (a[:128] + b[:128]) + (c[:128] + d[:128])
    if prev_ref is not None:
        total = total + prev_ref[...]
    sum_ref[...] = total
    most = jnp.maximum(jnp.maximum(a[128:], b[128:]), jnp.maximum(c[128:], d[128:]))
    most_ref[0] = jnp.max(most).astype(I32)
    more_ref[0] = (most_ref[0] > SLOTS).astype(I32)
    for g in range(CLASSES):
        out_ref[:, g * LANES : (g + 1) * LANES] = jnp.where(cls == g, total, 0.0).astype(BF16)


def params(mib):
    return pltpu.CompilerParams(vmem_limit_bytes=mib << 20)


def cost(flops, nbytes):
    return pl.CostEstimate(flops=flops, bytes_accessed=nbytes, transcendentals=0)


def swap(a, axis, partner):
    pairs = [(i, partner(i)) for i in range(lax.axis_size(axis))]
    return lax.ppermute(a, axis, pairs)


def across(i):
    return (i + 1 if i % 2 else i + 7) % 8


def beside(i):
    return i ^ 1


def round_body(start, prev, amplitudes, integrals, occ_irrep, vir_irrep, cd_list):
    n_occ, n_vir = occ_irrep.shape[0], vir_irrep.shape[0]
    rows, pairs = amplitudes.shape
    cols = integrals.shape[1]
    sds = jax.ShapeDtypeStruct
    occ = occ_irrep.reshape(1, n_occ)
    packed, hot, slot, symt, most, win = pl.pallas_call(
        functools.partial(pack_kernel, n_occ, n_vir),
        out_shape=(
            sds((rows, SLOTS), BF16),
            sds((pairs // CHUNK, WINDOW, CHUNK), BF16),
            sds((pairs // LANES, LANES), I32),
            sds((LANES, LANES), F32),
            sds((8, LANES), F32),
            sds((2 * pairs // CHUNK,), I32),
        ),
        in_specs=[SMEM, VMEM, VMEM, VMEM, VMEM],
        out_specs=(VMEM,) * 5 + (SMEM,),
        scratch_shapes=[
            pltpu.VMEM((1, LANES), I32),
            pltpu.VMEM((1, 10 * LANES), I32),
            pltpu.VMEM((2 * pairs // LANES, LANES), I32),
            pltpu.VMEM((rows, SLOTS + 3 * LANES), F32),
            pltpu.VMEM((rows, pairs), BF16),
        ],
        compiler_params=params(8),
        cost_estimate=cost(2 * rows * pairs * SLOTS, 6 << 20),
        name="pack",
    )(start, occ, vir_irrep, cd_list, amplitudes)

    parts = []
    count = cols // WIDTH
    quarter_of = pltpu.VMEM((pairs, WIDTH), BF16)
    for k in range(count):
        more = k + 1 < count
        out = (sds((SLOTS, WIDTH), BF16),) + more * (quarter_of,)
        scratch = [pltpu.VMEM((CHUNK, WIDTH), BF16), pltpu.VMEM((SLOTS + WINDOW, WIDTH), F32)]
        if k == 0:
            kernel, given, specs = first_weights_kernel, (integrals,), [ANY]
            scratch += [quarter_of, pltpu.SemaphoreType.DMA((pairs // CHUNK,))]
        else:
            kernel, given, specs = functools.partial(weights_kernel, k, more), (ready, integrals), [VMEM, ANY]
        if not more:
            given, specs = given[:1], specs[:1]
        part, *ready = pl.pallas_call(
            kernel,
            out_shape=out,
            in_specs=[SMEM, VMEM, VMEM, VMEM] + specs,
            out_specs=(VMEM,) * len(out),
            scratch_shapes=scratch + more * [pltpu.SemaphoreType.DMA],
            compiler_params=params(16),
            cost_estimate=cost(2 * WIDTH * pairs * SLOTS, 7 << 20),
            name="weights",
        )(win, hot, slot, symt, *given)
        parts.append(part)
        ready = ready[0] if more else None

    order = (0, 2, 3, 1)
    near = [packed] + [swap(packed, "x", lambda i, m=m: i ^ m) for m in order[1:]]
    mine = jnp.concatenate(near, axis=0)
    blocks, places = [mine], [(0, order)]
    far, close = mine, mine
    for k in range(1, 4):
        far, close = swap(close, "z", across), swap(far, "z", beside)
        blocks += [far, close]
        places += [(k, order), (-k, order)]
    blocks.append(swap(far, "z", beside))
    places.append((4, order))

    sums = sds((8, 128, LANES), F32)
    early = pl.pallas_call(
        functools.partial(early_kernel, n_occ, places[:-2]),
        out_shape=sums,
        in_specs=[VMEM] * (len(blocks) - 1 + len(parts)),
        out_specs=VMEM,
        scratch_shapes=[pltpu.VMEM((1, LANES), I32)],
        compiler_params=params(8),
        cost_estimate=cost(2 * 768 * cols * SLOTS, 4 << 20),
        name="early",
    )(occ, *blocks[:-2], *parts)
    keep, send = pl.pallas_call(
        functools.partial(product_kernel, n_occ, places[-2:]),
        out_shape=(sds((4, 136, LANES), F32),) * 2,
        in_specs=[VMEM] * (5 + len(parts)),
        out_specs=(VMEM,) * 2,
        scratch_shapes=[pltpu.VMEM((8, 128, LANES), F32), pltpu.VMEM((1, LANES), I32)],
        compiler_params=params(8),
        cost_estimate=cost(2 * 256 * cols * SLOTS, 1 << 20),
        name="product",
    )(occ, most, early, *blocks[-2:], *parts)

    got = swap(send, "core", beside)
    folded = pl.pallas_call(
        functools.partial(fold_kernel, order),
        out_shape=(sds((136, LANES), F32),) * 4,
        in_specs=[VMEM] * 2,
        out_specs=(VMEM,) * 4,
        compiler_params=params(8),
        name="fold",
    )(keep, got)
    arrived = [folded[0]] + [swap(f, "y", lambda i, m=m: i ^ m) for m, f in zip(order[1:], folded[1:])]
    kernel = functools.partial(finish_kernel, n_occ)
    if prev is None:
        kernel = lambda occ_ref, *refs: finish_kernel(n_occ, occ_ref, None, *refs)
    extra = () if prev is None else (prev,)
    return pl.pallas_call(
        kernel,
        out_shape=(sds((128, cols), BF16), sds((128, LANES), F32), sds((1,), I32), sds((1,), I32)),
        in_specs=[VMEM] * (5 + len(extra)),
        out_specs=(VMEM, VMEM, SMEM, SMEM),
        scratch_shapes=[pltpu.VMEM((1, LANES), I32)],
        compiler_params=params(8),
        name="finish",
    )(occ, *extra, *arrived)


def local(amplitudes, integrals, occ_irrep, vir_irrep, cd_list, ab_list):
    args = (amplitudes, integrals, occ_irrep, vir_irrep, cd_list)
    out, total, most, more_rounds = round_body(jnp.zeros((1,), I32), None, *args)

    def more(out, total, most):
        def body(state):
            k, _, total = state
            out, total, _, _ = round_body((k * SLOTS).reshape(1), total, *args)
            return k + 1, out, total

        return lax.while_loop(lambda s: s[0] * SLOTS < most[0], body, (jnp.int32(1), out, total))[1]

    return lax.switch(more_rounds[0], (lambda out, total, most: out, more), out, total, most)


def solution(mesh):
    fine = Mesh(mesh.devices.reshape(4, 2, 8, 4), ("y", "core", "z", "x"))
    owner, group = ("y", "core"), ("z", "x")
    return jax.shard_map(
        local,
        mesh=fine,
        in_specs=(P(group, owner), P(owner, group), P(), P(), P(None, owner), P(None, group)),
        out_specs=P(owner, group),
        check_vma=False,
    )
```
